32 devices in a mesh: gx: 4 (over y, core), gy: 2 (over x), gz: 4 (over z).
Axes of the slice: x: 2, y: 2, z: 4, core: 2. Of those that a mesh axis runs over, the one named last changes fastest.
Arguments:
- adjoint: float32 [64, 32, 512], P('gx', 'gy', 'gz'), may hold values from -6 to 6
- element_zone_index: int32 [16, 8, 128], P('gx', 'gy', 'gz'), may hold values from 0 to 7
- kappa_table: float32 [8], replicated, may hold values from 2 to 8
Outputs:
- prior_grad: float32 [64, 32, 512], P('gx', 'gy', 'gz')
- kappa_grad: float32 [16, 8, 128], P('gx', 'gy', 'gz')
The draws below stay inside these ranges and needn't reach their ends.
All inputs are finite; a program needn't handle non-finite values.
Results may differ from the reference program's by a relative error of at most 0.0001.
Values sent between devices are 32-bit elements; how exact they have to be, the bound alone decides.
A program may use at most 64 MiB of HBM per device.

```python
import math
import jax
import jax.numpy as jnp
import numpy as np
from jax import lax

MATERIAL_ZONES = 8
ELEMENTS_X = 16
ELEMENTS_Y = 8
ELEMENTS_Z = 128
NX = 64
NY = 32
NZ = 512


def with_ends(values, rng, low, largest):
    extent = values.shape
    place = [jax.random.randint(jax.random.fold_in(rng, axis), (), 0, extent[axis]) for axis in range(len(extent))]
    values = values.at[tuple(place)].set(low)
    longest = extent.index(max(extent))
    place[longest] = (place[longest] + 1) % extent[longest]
    return values.at[tuple(place)].set(largest)


def level_of(rng, dims, cuts, low, high):
    level = 1.0
    for dim, blocks in cuts:
        steps = jax.random.uniform(jax.random.fold_in(jax.random.fold_in(rng, 6), dim), (blocks,), jnp.float32, low / len(cuts), high / len(cuts))
        level = level * jnp.repeat(jnp.exp(steps), dims[dim] // blocks).reshape((-1,) + (1,) * (len(dims) - 1 - dim))
    return level


def gaussian(own_key, shape, width, bound, pieces=(), kind=jnp.bfloat16):
    values = jax.random.normal(own_key, shape, jnp.float32) * width
    if len(pieces) > 0:
        values = level_of(own_key, shape, pieces, -0.22, 0.18) * values
    return jnp.clip(values, min=-bound, max=bound).astype(kind)


def setup_inputs(seed: int = 0) -> dict:
    key_of = jax.random.split(jax.random.key(seed), 4)
    adjoint = gaussian(key_of[0], (NX, NY, NZ), 1.0, 6.0, ((0, 4), (1, 2), (2, 4)), jnp.float32)
    element_zone_index = with_ends(jax.random.randint(key_of[1], (ELEMENTS_X, ELEMENTS_Y, ELEMENTS_Z), 0, MATERIAL_ZONES), jax.random.fold_in(key_of[1], 1), 0, MATERIAL_ZONES - 1).astype(jnp.int32)
    kappa_table = jnp.clip(jnp.exp(jax.random.uniform(key_of[2], (MATERIAL_ZONES,), jnp.float32, math.log(2.0), math.log(8.0))), 2.0, 8.0)
    return {"adjoint": adjoint, "element_zone_index": element_zone_index, "kappa_table": kappa_table}


def gll_tables():
    points = np.array([-1.0, -math.sqrt(3.0 / 7.0), 0.0, math.sqrt(3.0 / 7.0), 1.0])
    weights = np.array([0.1, 49.0 / 90.0, 32.0 / 45.0, 49.0 / 90.0, 0.1])
    scales = np.array([np.prod([points[row_pos] - points[other] for other in range(5) if other != row_pos]) for row_pos in range(5)])
    derivative = np.zeros((5, 5))
    for row_pos in range(5):
        for col_pos in range(5):
            if row_pos != col_pos:
                derivative[row_pos, col_pos] = scales[row_pos] / scales[col_pos] / (points[row_pos] - points[col_pos])
        derivative[row_pos, row_pos] = -np.sum(derivative[row_pos])
    stiffness = derivative.T @ (weights[:, None] * derivative)
    return (weights, stiffness)

def windows(values):
    count = values.shape[0] // 4
    padded = jnp.concatenate([values, jnp.zeros((1,) + values.shape[1:], values.dtype)], axis=0)
    lower = padded[:4 * count].reshape((count, 4) + values.shape[1:])
    extra = padded[4::4]
    return jnp.concatenate([lower, extra[:, None]], axis=1)

def assemble(parts):
    count = parts.shape[0]
    main_part = parts[:, :4].reshape((4 * count,) + parts.shape[2:])
    return main_part.at[4::4].add(parts[:-1, 4])

def along(values, axis_pos, func):
    moved = jnp.moveaxis(values, axis_pos, 0)
    return jnp.moveaxis(func(moved), 0, axis_pos)

def stiff_front(values):
    weights, stiffness = gll_tables()
    local = jnp.einsum('ab,eb...->ea...', jnp.asarray(stiffness, jnp.float32), windows(values), precision=lax.Precision.HIGHEST)
    return assemble(local)

def spread_front(element_vals):
    weights, stiffness = gll_tables()
    wvec = jnp.asarray(weights, jnp.float32)
    local = element_vals[:, None] * wvec.reshape((1, 5) + (1,) * (element_vals.ndim - 1))
    return assemble(local)

def restrict_front(values):
    weights, stiffness = gll_tables()
    return jnp.einsum('a,ea...->e...', jnp.asarray(weights, jnp.float32), windows(values), precision=lax.Precision.HIGHEST)

def diagonal_mass_line(count):
    return spread_front(jnp.ones((count,), jnp.float32))

def reference(adjoint, element_zone_index, kappa_table):
    kappa = kappa_table[element_zone_index]
    lumped_x = diagonal_mass_line(ELEMENTS_X)
    lumped_y = diagonal_mass_line(ELEMENTS_Y)
    diagonal_mass_depth = diagonal_mass_line(ELEMENTS_Z)
    mass_kappa = kappa * kappa
    for axis_pos in range(3):
        mass_kappa = along(mass_kappa, axis_pos, spread_front)
    lumped = lumped_x[:, None, None] * lumped_y[None, :, None] * diagonal_mass_depth[None, None, :]

    def operate(values):
        result = mass_kappa * values
        result = result + stiff_front(values) * lumped_y[None, :, None] * diagonal_mass_depth[None, None, :]
        result = result + along(values, 1, stiff_front) * lumped_x[:, None, None] * diagonal_mass_depth[None, None, :]
        result = result + along(values, 2, stiff_front) * lumped_x[:, None, None] * lumped_y[None, :, None]
        return result
    scaled = operate(adjoint) / lumped
    prior_grad = 0.001 * operate(scaled)
    product = adjoint * scaled
    for axis_pos in range(3):
        product = along(product, axis_pos, restrict_front)
    kappa_grad = 0.002 * kappa * product
    return (prior_grad, kappa_grad)
```

```python
import functools
import itertools
import math

import jax
import jax.numpy as jnp
import numpy as np
from jax import lax
from jax.experimental import pallas as pl
from jax.experimental.pallas import tpu as pltpu
from jax.sharding import PartitionSpec as P

AXES = ("gx", "gy", "gz")
HIGHEST = lax.Precision.HIGHEST
OFFSETS = [o for o in itertools.product((0, 1), repeat=3) if sum(o) > 0]


def gll_tables():
    points = np.array([-1.0, -math.sqrt(3.0 / 7.0), 0.0, math.sqrt(3.0 / 7.0), 1.0])
    weights = np.array([0.1, 49.0 / 90.0, 32.0 / 45.0, 49.0 / 90.0, 0.1])
    scales = np.array(
        [np.prod([points[r] - points[o] for o in range(5) if o != r]) for r in range(5)]
    )
    derivative = np.zeros((5, 5))
    for r in range(5):
        for c in range(5):
            if r != c:
                derivative[r, c] = scales[r] / scales[c] / (points[r] - points[c])
        derivative[r, r] = -np.sum(derivative[r])
    return weights, derivative.T @ (weights[:, None] * derivative)


WEIGHTS, STIFF = gll_tables()
LUMPED = np.array([2 * WEIGHTS[0], WEIGHTS[1], WEIGHTS[2], WEIGHTS[3]])
WN = WEIGHTS[:4] / LUMPED
WN0 = float(WEIGHTS[4] / LUMPED[0])
END_DIAG = float(STIFF[4, 4] / LUMPED[0])


def constants(ez):
    nodes = 4 * ez
    stiff_z = np.zeros((nodes, nodes))
    zexp = np.zeros((ez, 2 * nodes))
    zred = np.zeros((2, nodes, ez))
    for e in range(ez):
        for a in range(5):
            k = 4 * e + a
            if k < nodes:
                zexp[e, k] += WEIGHTS[a] / LUMPED[a % 4]
                zred[0, k, e] += WEIGHTS[a]
                for b in range(5):
                    if 4 * e + b < nodes:
                        stiff_z[4 * e + b, k] += STIFF[a, b] / LUMPED[a % 4]
    zexp[ez - 1, nodes] = WN0
    zred[1, 0, ez - 1] = WEIGHTS[4]
    return tuple(np.asarray(c, np.float32) for c in (stiff_z, zexp, zred))


def dot(a, b):
    return jnp.dot(a, b, precision=HIGHEST, preferred_element_type=jnp.float32)


def weighted(layers, coef):
    total = None
    for n, c in sorted(coef.items()):
        term = layers[n] * jnp.float32(c)
        total = term if total is None else total + term
    return total


def line_terms(layers, elems):
    out = []
    for i in range(4 * elems):
        e, a = divmod(i, 4)
        coef = {}
        for b in range(5):
            coef[4 * e + b] = STIFF[a, b] / LUMPED[a]
        if a == 0 and e > 0:
            for b in range(5):
                n = 4 * e - 4 + b
                coef[n] = coef.get(n, 0.0) + STIFF[4, b] / LUMPED[0]
        out.append(weighted(layers, {n: c for n, c in coef.items() if n < 4 * elems}))
    return out


def last_partial(layers, elems):
    return weighted(layers, {4 * elems - 4 + b: STIFF[4, b] / LUMPED[0] for b in range(4)})


def element_lines(layers, elems):
    out = []
    for e in range(elems):
        coef = {4 * e + a: WEIGHTS[a] for a in range(5) if 4 * e + a < 4 * elems}
        out.append(weighted(layers, coef))
    out.append(layers[0] * jnp.float32(WEIGHTS[4]))
    return out


def pattern(index, values):
    total = jnp.full(index.shape, values[-1], jnp.float32)
    for a in range(len(values) - 1):
        total = jnp.where(index == a, jnp.float32(values[a]), total)
    return total


def kernel(sizes, elems, *refs):
    (
        adj_hbm, zones_hbm, table_hbm, stiff_hbm, zexp_hbm, zred_hbm,
        prior, kgrad,
        adj, zones, table, stiff_z, zexp, zred,
        scaled, work, diag, lines, face_send, face_recv, z_send, z_recv,
        t_send, t_recv, e_send, e_recv, load_sem, send_sem, recv_sem,
    ) = refs
    ex, ey, ez = elems
    nx, ny, nz = 4 * ex, 4 * ey, 4 * ez
    tiles = nx * ny // 8
    loads = [
        pltpu.make_async_copy(src, dst, load_sem.at[n])
        for n, (src, dst) in enumerate(
            ((zones_hbm, zones), (zexp_hbm, zexp), (adj_hbm, adj), (stiff_hbm, stiff_z), (zred_hbm, zred), (table_hbm, table))
        )
    ]
    for copy in loads:
        copy.start()
    me = tuple(lax.axis_index(a) for a in AXES)
    low = tuple(jnp.minimum(m, 1) for m in me)
    high = tuple(jnp.minimum(s - 1 - m, 1) for m, s in zip(me, sizes))

    def exists(flags, off):
        ok = None
        for f, o in zip(flags, off):
            if o:
                ok = f if ok is None else ok * f
        return ok == 1

    def shifted(off, sign):
        return {a: m + sign * o for a, m, o in zip(AXES, me, off) if o}

    barrier = pltpu.get_barrier_semaphore()
    for off in reversed(OFFSETS):
        for flags, sign in ((high, 1), (low, -1)):
            @pl.when(exists(flags, off))
            def _():
                pl.semaphore_signal(
                    barrier, inc=1, device_id=shifted(off, sign),
                    device_id_type=pl.DeviceIdType.MESH,
                )

    started = []

    def message(src, dst, num, off, sign):
        copy = pltpu.make_async_remote_copy(
            src_ref=src, dst_ref=dst, send_sem=send_sem.at[num], recv_sem=recv_sem.at[num],
            device_id=shifted(off, sign), device_id_type=pl.DeviceIdType.MESH,
        )
        to, come = (high, low) if sign > 0 else (low, high)
        started.append((copy, to, off))

        @pl.when(exists(to, off))
        def _():
            copy.start()

        def arrived():
            @pl.when(exists(come, off))
            def _():
                copy.wait_recv()

        return arrived

    has_low = [f == 1 for f in low]
    has_high = [f == 1 for f in high]
    zero, one = jnp.float32(0.0), jnp.float32(1.0)
    first = [jnp.where(h, one, jnp.float32(2.0)) for h in has_low]
    lane = lax.broadcasted_iota(jnp.int32, (1, nz), 1)
    lane8 = lax.broadcasted_iota(jnp.int32, (8, nz), 1)
    row = lax.broadcasted_iota(jnp.int32, (ny, nz), 0)
    col = lax.broadcasted_iota(jnp.int32, (ny, nz), 1)
    ends = list(STIFF[:4, 4] / LUMPED)
    sends = list(STIFF[4, :4] / LUMPED[0])
    take_first = jnp.where(lane == 0, one, zero)
    take_last = pattern(lane - (nz - 4), ends + [0.0])
    send_last = pattern(lane - (nz - 4), sends + [0.0])

    def xs(ref, i):
        return ref[i * ny : (i + 1) * ny, :]

    def ys(ref, j):
        return ref[pl.ds(j, nx, stride=ny), :]

    def fill_faces(src, phase):
        face_send[phase, 0] = last_partial({i: xs(src, i) for i in range(nx - 4, nx)}, ex)
        face_send[phase, 1] = last_partial({j: ys(src, j) for j in range(ny - 4, ny)}, ey)
        face_send[phase, 2] = ys(src, 0)
        packed = jnp.zeros((8, nz), jnp.float32)
        for v in range(tiles):
            tile = src[8 * v : 8 * v + 8, :]
            total = jnp.sum(tile * send_last, axis=1, keepdims=True)
            packed = jnp.where(lane8 == v, total, packed)
            packed = jnp.where(lane8 == tiles + v, tile[:, 0:1], packed)
        z_send[phase] = packed

    def send_faces(src, phase):
        base = 6 * phase
        return [
            message(z_send.at[phase], z_recv.at[phase, 0], base + 4, (0, 0, 1), 1),
            message(z_send.at[phase], z_recv.at[phase, 1], base + 5, (0, 0, 1), -1),
            message(face_send.at[phase, 1], face_recv.at[phase, 2], base + 2, (0, 1, 0), 1),
            message(face_send.at[phase, 2], face_recv.at[phase, 3], base + 3, (0, 1, 0), -1),
            message(face_send.at[phase, 0], face_recv.at[phase, 0], base, (1, 0, 0), 1),
            message(src.at[0:ny], face_recv.at[phase, 1], base + 1, (1, 0, 0), -1),
        ]

    def own_terms(src):
        along_z = dot(src[...], stiff_z[...]) * jnp.where(lane == 0, first[2], one)
        ylines = line_terms([ys(src, j) for j in range(ny)], ey)
        for j in range(ny):
            work[pl.ds(j, nx, stride=ny), :] = ylines[j] * first[1] if j == 0 else ylines[j]
        xlines = line_terms([xs(src, i) for i in range(nx)], ex)
        for i in range(nx):
            term = xlines[i] * first[0] if i == 0 else xlines[i]
            work[i * ny : (i + 1) * ny, :] += term + along_z[i * ny : (i + 1) * ny, :]

    def halo_terms(phase):
        py = jnp.where(has_low[1], face_recv[phase, 2], zero)
        uy = jnp.where(has_high[1], face_recv[phase, 3], zero)
        work[pl.ds(0, nx, stride=ny), :] += py
        for a in range(4):
            work[pl.ds(ny - 4 + a, nx, stride=ny), :] += uy * jnp.float32(ends[a])
        px = jnp.where(has_low[0], face_recv[phase, 0], zero)
        ux = jnp.where(has_high[0], face_recv[phase, 1], zero)
        zlow = jnp.where(has_low[2], z_recv[phase, 0], zero)
        zhigh = jnp.where(has_high[2], z_recv[phase, 1], zero)

        def layer(i):
            parts = []
            for v in range(i * ny // 8, (i + 1) * ny // 8):
                parts.append(
                    zlow[:, v : v + 1] * take_first
                    + zhigh[:, tiles + v : tiles + v + 1] * take_last
                )
            total = jnp.concatenate(parts, axis=0)
            if i == 0:
                total = total + px
            if i >= nx - 4:
                total = total + ux * jnp.float32(ends[i - nx + 4])
            return total

        return layer

    def kappa_of(values):
        kappa = jnp.zeros(values.shape, jnp.float32)
        for zone in range(table.shape[0]):
            kappa = jnp.where(values == zone, table[zone], kappa)
        return kappa

    block = ex * ey
    loads[5].wait()
    loads[0].wait()
    loads[1].wait()
    own_kappa = [kappa_of(zones[e]) for e in range(ex)]
    kappa_sq = jnp.concatenate([k * k for k in own_kappa], axis=0)
    spread_z = dot(kappa_sq, zexp[...])
    t_send[0] = spread_z[:, :nz]
    t_send[1] = spread_z[:, nz:]
    ups = functools.reduce(lambda a, b: a * b, [1 + f for f in high])
    downs = functools.reduce(lambda a, b: a * b, [1 + f for f in low])
    pl.semaphore_wait(barrier, ups + downs - 2)
    t_got = []
    for n, off in reversed(list(enumerate(OFFSETS))):
        t_got.append(message(t_send.at[off[2]], t_recv.at[n], 12 + n, off, 1))
    loads[2].wait()
    fill_faces(adj, 0)
    got = send_faces(adj, 0)

    loads[3].wait()
    own_terms(adj)
    at_y, at_z = row == 0, col == 0
    doubled = jnp.where(at_y, first[1], one) * jnp.where(at_z, first[2], one)
    end_y = jnp.where(at_y, jnp.where(has_low[1], jnp.float32(END_DIAG), zero), zero)
    end_yz = end_y + jnp.where(at_z, jnp.where(has_low[2], jnp.float32(END_DIAG), zero), zero)
    end_x = jnp.where(has_low[0], jnp.float32(END_DIAG), zero)
    mass_yz = pattern(lax.rem(row, 4), list(LUMPED)) * pattern(lax.rem(col, 4), list(LUMPED))
    mass_yz = mass_yz * jnp.float32(0.001) / doubled
    y_coef = []
    for f in range(-1, ey):
        local = row - 4 * f
        y_coef.append(pattern(local, list(WN) + [WN0, 0.0]) * doubled)

    for w in got:
        w()
    layer = halo_terms(0)
    for i in range(nx):
        work[i * ny : (i + 1) * ny, :] += layer(i)

    for w in t_got:
        w()

    def spread_at(sx, sy):
        total = None
        for sz in range(2):
            off = (sx, sy, sz)
            if off == (0, 0, 0):
                part = t_send[0]
            else:
                part = jnp.where(exists(low, off), t_recv[OFFSETS.index(off)], zero)
            total = part if total is None else total + part
        return total

    slots = {(sx, sy): spread_at(sx, sy) for sx in range(2) for sy in range(2)}
    columns = []
    for e in range(-1, ex):
        total = None
        for f in range(-1, ey):
            source = slots[(int(e < 0), int(f < 0))]
            r = (e % ex) * ey + f % ey
            term = source[r : r + 1, :] * y_coef[f + 1]
            total = term if total is None else total + term
        columns.append(total)
    for i in range(nx):
        e, a = divmod(i, 4)
        if a == 0:
            mass = (columns[e + 1] + columns[e]) * jnp.float32(WN0)
        else:
            mass = columns[e + 1] * jnp.float32(WN[a])
        value = mass * first[0] + (end_yz + end_x) if i == 0 else mass + end_yz
        rows = slice(i * ny, (i + 1) * ny)
        diag[rows, :] = value
        scaled[rows, :] = work[rows, :] + value * adj[rows, :]

    ysums = element_lines([ys(adj, j) * ys(scaled, j) for j in range(ny)], ey)
    for f in range(8):
        lines[f * nx : (f + 1) * nx, :] = ysums[f] if f <= ey else jnp.zeros((nx, nz), jnp.float32)
    xsums = element_lines([lines[pl.ds(i, 8, stride=nx), :] for i in range(nx)], ex)
    xsums = jnp.concatenate(xsums, axis=0)
    loads[4].wait()
    for sz in range(2):
        e_send[sz] = dot(xsums, zred[sz])
    e_got = []
    for n, off in reversed(list(enumerate(OFFSETS))):
        rows = pl.ds(8 * ex, 8) if off[0] else pl.ds(0, 8 * ex)
        e_got.append(message(e_send.at[off[2], rows], e_recv.at[n, rows], 19 + n, off, -1))

    fill_faces(scaled, 1)
    got = send_faces(scaled, 1)

    own_terms(scaled)
    work[...] += diag[...] * scaled[...]
    for w in got:
        w()
    layer = halo_terms(1)
    for i in range(nx):
        rows = slice(i * ny, (i + 1) * ny)
        factor = mass_yz * jnp.float32(LUMPED[i % 4])
        if i == 0:
            factor = factor / first[0]
        prior[rows, :] = (work[rows, :] + layer(i)) * factor

    for copy, to, off in started:
        @pl.when(exists(to, off))
        def _():
            copy.wait_send()

    for w in e_got:
        w()
    row8 = lax.broadcasted_iota(jnp.int32, (8, ez), 0)
    for e in range(ex):
        total = e_send[0, 8 * e : 8 * e + 8]
        above = jnp.zeros((8, ez), jnp.float32)
        for n, off in enumerate(OFFSETS):
            if off[0] and e < ex - 1:
                continue
            start = 8 * ex if off[0] else 8 * e
            part = jnp.where(exists(high, off), e_recv[n, start : start + 8], zero)
            if off[1]:
                above = above + part
            else:
                total = total + part
        total = total + jnp.where(row8 == ey - 1, pltpu.roll(above, 7, 0), zero)
        kgrad[e] = total[:ey] * (own_kappa[e] * jnp.float32(0.002))


def finish(prior, kgrad, prior_out, kgrad_out, sem):
    copies = [
        pltpu.make_async_copy(src, dst, sem.at[n])
        for n, (src, dst) in enumerate(((prior, prior_out), (kgrad, kgrad_out)))
    ]
    for copy in copies:
        copy.start()
    for copy in copies:
        copy.wait()


def on_device(sizes, adjoint, element_zone_index, kappa_table):
    nx, ny, nz = adjoint.shape
    elems = ex, ey, ez = element_zone_index.shape
    consts = [jnp.asarray(c) for c in constants(ez)]
    f32 = jnp.float32
    vmem = pl.BlockSpec(memory_space=pltpu.VMEM)
    hbm = pl.BlockSpec(memory_space=pltpu.HBM)
    prior, kgrad = pl.pallas_call(
        functools.partial(kernel, sizes, elems),
        out_shape=(pltpu.VMEM((nx * ny, nz), f32), pltpu.VMEM((ex, ey, ez), f32)),
        in_specs=[hbm] * (3 + len(consts)),
        out_specs=(vmem, vmem),
        scratch_shapes=[
            pltpu.VMEM((nx * ny, nz), f32),
            pltpu.VMEM((ex, ey, ez), jnp.int32),
            pltpu.SMEM(kappa_table.shape, f32),
            pltpu.VMEM(consts[0].shape, f32),
            pltpu.VMEM(consts[1].shape, f32),
            pltpu.VMEM(consts[2].shape, f32),
            pltpu.VMEM((nx * ny, nz), f32),
            pltpu.VMEM((nx * ny, nz), f32),
            pltpu.VMEM((nx * ny, nz), f32),
            pltpu.VMEM((8 * nx, nz), f32),
            pltpu.VMEM((2, 3, ny, nz), f32),
            pltpu.VMEM((2, 4, ny, nz), f32),
            pltpu.VMEM((2, 8, nz), f32),
            pltpu.VMEM((2, 2, 8, nz), f32),
            pltpu.VMEM((2, ex * ey, nz), f32),
            pltpu.VMEM((7, ex * ey, nz), f32),
            pltpu.VMEM((2, 8 * ex + 8, ez), f32),
            pltpu.VMEM((7, 8 * ex + 8, ez), f32),
            pltpu.SemaphoreType.DMA((6,)),
            pltpu.SemaphoreType.DMA((26,)),
            pltpu.SemaphoreType.DMA((26,)),
        ],
        compiler_params=pltpu.CompilerParams(
            collective_id=0, has_side_effects=True
        ),
        name="bilaplacian",
    )(adjoint.reshape(nx * ny, nz), element_zone_index, kappa_table, *consts)
    prior, kgrad = pl.pallas_call(
        finish,
        out_shape=(
            jax.ShapeDtypeStruct((nx * ny, nz), f32),
            jax.ShapeDtypeStruct((ex, ey, ez), f32),
        ),
        in_specs=[vmem, vmem],
        out_specs=(hbm, hbm),
        scratch_shapes=[pltpu.SemaphoreType.DMA((2,))],
        name="finish",
    )(*(pltpu.with_memory_space_constraint(r, pltpu.VMEM) for r in (prior, kgrad)))
    return prior.reshape(nx, ny, nz), kgrad


def solution(mesh):
    sizes = tuple(mesh.shape[a] for a in AXES)
    return jax.shard_map(
        functools.partial(on_device, sizes), mesh=mesh,
        in_specs=(P("gx", "gy", "gz"), P("gx", "gy", "gz"), P()),
        out_specs=(P("gx", "gy", "gz"), P("gx", "gy", "gz")), check_vma=False,
    )
```

```python
import functools
import itertools
import math

import jax
import jax.numpy as jnp
import numpy as np
from jax import lax
from jax.experimental import pallas as pl
from jax.experimental.pallas import tpu as pltpu
from jax.sharding import PartitionSpec as P

AXES = ("gx", "gy", "gz")
HIGHEST = lax.Precision.HIGHEST
OFFSETS = [o for o in itertools.product((0, 1), repeat=3) if sum(o) > 0]


def gll_tables():
    points = np.array([-1.0, -math.sqrt(3.0 / 7.0), 0.0, math.sqrt(3.0 / 7.0), 1.0])
    weights = np.array([0.1, 49.0 / 90.0, 32.0 / 45.0, 49.0 / 90.0, 0.1])
    scales = np.array(
        [np.prod([points[r] - points[o] for o in range(5) if o != r]) for r in range(5)]
    )
    derivative = np.zeros((5, 5))
    for r in range(5):
        for c in range(5):
            if r != c:
                derivative[r, c] = scales[r] / scales[c] / (points[r] - points[c])
        derivative[r, r] = -np.sum(derivative[r])
    return weights, derivative.T @ (weights[:, None] * derivative)


WEIGHTS, STIFF = gll_tables()
LUMPED = np.array([2 * WEIGHTS[0], WEIGHTS[1], WEIGHTS[2], WEIGHTS[3]])
WN = WEIGHTS[:4] / LUMPED
WN0 = float(WEIGHTS[4] / LUMPED[0])
END_DIAG = float(STIFF[4, 4] / LUMPED[0])


def constants(ez):
    nodes = 4 * ez
    stiff_z = np.zeros((nodes, nodes))
    zexp = np.zeros((ez, nodes))
    zred = np.zeros((nodes, ez))
    for e in range(ez):
        for a in range(5):
            k = 4 * e + a
            if k < nodes:
                zexp[e, k] += WEIGHTS[a] / LUMPED[a % 4]
                zred[k, e] += WEIGHTS[a]
                for b in range(5):
                    if 4 * e + b < nodes:
                        stiff_z[4 * e + b, k] += STIFF[a, b] / LUMPED[a % 4]
    return tuple(np.asarray(c, np.float32) for c in (stiff_z, zexp, zred))


def dot(a, b):
    return jnp.dot(a, b, precision=HIGHEST, preferred_element_type=jnp.float32)


def weighted(layers, coef):
    total = None
    for n, c in sorted(coef.items()):
        term = layers[n] * jnp.float32(c)
        total = term if total is None else total + term
    return total


def line_terms(layers, elems):
    out = []
    for i in range(4 * elems):
        e, a = divmod(i, 4)
        coef = {}
        for b in range(5):
            coef[4 * e + b] = STIFF[a, b] / LUMPED[a]
        if a == 0 and e > 0:
            for b in range(5):
                n = 4 * e - 4 + b
                coef[n] = coef.get(n, 0.0) + STIFF[4, b] / LUMPED[0]
        out.append(weighted(layers, {n: c for n, c in coef.items() if n < 4 * elems}))
    return out


def last_partial(layers, elems):
    return weighted(layers, {4 * elems - 4 + b: STIFF[4, b] / LUMPED[0] for b in range(4)})


def element_lines(layers, elems):
    out = []
    for e in range(elems):
        coef = {4 * e + a: WEIGHTS[a] for a in range(5) if 4 * e + a < 4 * elems}
        out.append(weighted(layers, coef))
    out.append(layers[0] * jnp.float32(WEIGHTS[4]))
    return out


def pattern(index, values):
    total = jnp.full(index.shape, values[-1], jnp.float32)
    for a in range(len(values) - 1):
        total = jnp.where(index == a, jnp.float32(values[a]), total)
    return total


def kernel(sizes, elems, *refs):
    (
        adj_hbm, zones_hbm, table_hbm, stiff_hbm, zexp_hbm, zred_hbm,
        prior, kgrad,
        adj, zones, table, stiff_z, zexp, zred,
        scaled, work, diag, lines, face_send, face_recv, z_send, z_recv,
        tx_send, ty_send, txy_send, tx_recv, ty_recv, txy_recv,
        e_own, ey_send, exy_send, ez_send, ezy_send,
        ex_recv, ey_recv, exy_recv, ez_recv, ezy_recv, load_sem, send_sem, recv_sem,
    ) = refs
    ex, ey, ez = elems
    nx, ny, nz = 4 * ex, 4 * ey, 4 * ez
    tiles = nx * ny // 8
    loads = [
        pltpu.make_async_copy(src, dst, load_sem.at[n])
        for n, (src, dst) in enumerate(
            ((zones_hbm, zones), (zexp_hbm, zexp), (adj_hbm, adj), (stiff_hbm, stiff_z), (zred_hbm, zred), (table_hbm, table))
        )
    ]
    for n in (2, 0, 5, 1, 3, 4):
        loads[n].start()
    me = tuple(lax.axis_index(a) for a in AXES)
    low = tuple(jnp.minimum(m, 1) for m in me)
    high = tuple(jnp.minimum(s - 1 - m, 1) for m, s in zip(me, sizes))

    def exists(flags, off):
        ok = None
        for f, o in zip(flags, off):
            if o:
                ok = f if ok is None else ok * f
        return ok == 1

    def shifted(off, sign):
        return {a: m + sign * o for a, m, o in zip(AXES, me, off) if o}

    barrier = pltpu.get_barrier_semaphore()
    for off in reversed(OFFSETS):
        for flags, sign in ((high, 1), (low, -1)):
            @pl.when(exists(flags, off))
            def _():
                pl.semaphore_signal(
                    barrier, inc=1, device_id=shifted(off, sign),
                    device_id_type=pl.DeviceIdType.MESH,
                )

    started = []

    def message(src, dst, num, off, sign):
        copy = pltpu.make_async_remote_copy(
            src_ref=src, dst_ref=dst, send_sem=send_sem.at[num], recv_sem=recv_sem.at[num],
            device_id=shifted(off, sign), device_id_type=pl.DeviceIdType.MESH,
        )
        to, come = (high, low) if sign > 0 else (low, high)
        started.append((copy, to, off))

        @pl.when(exists(to, off))
        def _():
            copy.start()

        def arrived():
            @pl.when(exists(come, off))
            def _():
                copy.wait_recv()

        return arrived

    has_low = [f == 1 for f in low]
    has_high = [f == 1 for f in high]
    zero, one = jnp.float32(0.0), jnp.float32(1.0)
    first = [jnp.where(h, one, jnp.float32(2.0)) for h in has_low]
    lane = lax.broadcasted_iota(jnp.int32, (1, nz), 1)
    lane8 = lax.broadcasted_iota(jnp.int32, (8, nz), 1)
    row = lax.broadcasted_iota(jnp.int32, (ny, nz), 0)
    col = lax.broadcasted_iota(jnp.int32, (ny, nz), 1)
    ends = list(STIFF[:4, 4] / LUMPED)
    sends = list(STIFF[4, :4] / LUMPED[0])
    take_first = jnp.where(lane == 0, one, zero)
    take_last = pattern(lane - (nz - 4), ends + [0.0])
    send_last = pattern(lane - (nz - 4), sends + [0.0])

    def xs(ref, i):
        return ref[i * ny : (i + 1) * ny, :]

    def ys(ref, j):
        return ref[pl.ds(j, nx, stride=ny), :]

    def fill_faces(src, phase, extra=()):
        face_send[phase, 0] = last_partial({i: xs(src, i) for i in range(nx - 4, nx)}, ex)
        face_send[phase, 1] = last_partial({j: ys(src, j) for j in range(ny - 4, ny)}, ey)
        face_send[phase, 2] = ys(src, 0)
        packed = jnp.zeros((8, nz), jnp.float32)
        for v in range(tiles):
            tile = src[8 * v : 8 * v + 8, :]
            total = jnp.sum(tile * send_last, axis=1, keepdims=True)
            packed = jnp.where(lane8 == v, total, packed)
            packed = jnp.where(lane8 == tiles + v, tile[:, 0:1], packed)
        for n, column in enumerate(extra):
            packed = jnp.where(lane8 == 2 * tiles + n, column, packed)
        z_send[phase] = packed

    def send_faces(src, phase):
        base = 6 * phase
        return [
            message(z_send.at[phase], z_recv.at[phase, 0], base + 4, (0, 0, 1), 1),
            message(z_send.at[phase], z_recv.at[phase, 1], base + 5, (0, 0, 1), -1),
            message(face_send.at[phase, 1], face_recv.at[phase, 2], base + 2, (0, 1, 0), 1),
            message(face_send.at[phase, 2], face_recv.at[phase, 3], base + 3, (0, 1, 0), -1),
            message(face_send.at[phase, 0], face_recv.at[phase, 0], base, (1, 0, 0), 1),
            message(src.at[0:ny], face_recv.at[phase, 1], base + 1, (1, 0, 0), -1),
        ]

    def own_terms(src):
        along_z = dot(src[...], stiff_z[...]) * jnp.where(lane == 0, first[2], one)
        ylines = line_terms([ys(src, j) for j in range(ny)], ey)
        for j in range(ny):
            work[pl.ds(j, nx, stride=ny), :] = ylines[j] * first[1] if j == 0 else ylines[j]
        xlines = line_terms([xs(src, i) for i in range(nx)], ex)
        for i in range(nx):
            term = xlines[i] * first[0] if i == 0 else xlines[i]
            work[i * ny : (i + 1) * ny, :] += term + along_z[i * ny : (i + 1) * ny, :]

    def halo_terms(phase):
        py = jnp.where(has_low[1], face_recv[phase, 2], zero)
        uy = jnp.where(has_high[1], face_recv[phase, 3], zero)
        work[pl.ds(0, nx, stride=ny), :] += py
        for a in range(4):
            work[pl.ds(ny - 4 + a, nx, stride=ny), :] += uy * jnp.float32(ends[a])
        px = jnp.where(has_low[0], face_recv[phase, 0], zero)
        ux = jnp.where(has_high[0], face_recv[phase, 1], zero)
        zlow = jnp.where(has_low[2], z_recv[phase, 0], zero)
        zhigh = jnp.where(has_high[2], z_recv[phase, 1], zero)

        def layer(i):
            parts = []
            for v in range(i * ny // 8, (i + 1) * ny // 8):
                parts.append(
                    zlow[:, v : v + 1] * take_first
                    + zhigh[:, tiles + v : tiles + v + 1] * take_last
                )
            total = jnp.concatenate(parts, axis=0)
            if i == 0:
                total = total + px
            if i >= nx - 4:
                total = total + ux * jnp.float32(ends[i - nx + 4])
            return total

        return layer

    def kappa_of(values):
        kappa = jnp.zeros(values.shape, jnp.float32)
        for zone in range(table.shape[0]):
            kappa = jnp.where(values == zone, table[zone], kappa)
        return kappa

    block = ex * ey
    loads[5].wait()
    loads[0].wait()
    loads[1].wait()
    own_kappa = [kappa_of(zones[e]) for e in range(ex)]
    kappa_sq = jnp.concatenate([k * k for k in own_kappa], axis=0)
    spread_z = dot(kappa_sq, zexp[...])
    end_z = kappa_sq[:, ez - 1 :] * jnp.float32(WN0)
    for sz, rows in enumerate((spread_z, end_z * take_first)):
        tx_send[sz] = rows[block - ey :]
        for e in range(ex):
            ty_send[sz, e : e + 1] = rows[(e + 1) * ey - 1 : (e + 1) * ey]
        txy_send[sz] = rows[block - 1 :]
    loads[2].wait()
    fill_faces(adj, 0, [end_z[8 * n : 8 * n + 8] for n in range(block // 8)])
    ups = functools.reduce(lambda a, b: a * b, [1 + f for f in high])
    downs = functools.reduce(lambda a, b: a * b, [1 + f for f in low])
    pl.semaphore_wait(barrier, ups + downs - 2)
    t_got = []
    for n, off in reversed(list(enumerate(OFFSETS))):
        if off == (0, 0, 1):
            continue
        send, recv = {(1, 0): (tx_send, tx_recv), (0, 1): (ty_send, ty_recv), (1, 1): (txy_send, txy_recv)}[off[:2]]
        t_got.append(message(send.at[off[2]], recv.at[off[2]], 12 + n, off, 1))
    got = send_faces(adj, 0)

    loads[3].wait()
    own_terms(adj)
    at_y, at_z = row == 0, col == 0
    doubled = jnp.where(at_y, first[1], one) * jnp.where(at_z, first[2], one)
    end_y = jnp.where(at_y, jnp.where(has_low[1], jnp.float32(END_DIAG), zero), zero)
    end_yz = end_y + jnp.where(at_z, jnp.where(has_low[2], jnp.float32(END_DIAG), zero), zero)
    end_x = jnp.where(has_low[0], jnp.float32(END_DIAG), zero)
    mass_yz = pattern(lax.rem(row, 4), list(LUMPED)) * pattern(lax.rem(col, 4), list(LUMPED))
    mass_yz = mass_yz * jnp.float32(0.001) / doubled
    y_coef = []
    for f in range(-1, ey):
        local = row - 4 * f
        y_coef.append(pattern(local, list(WN) + [WN0, 0.0]) * doubled)

    for w in got:
        w()
    layer = halo_terms(0)
    for i in range(nx):
        work[i * ny : (i + 1) * ny, :] += layer(i)

    for w in t_got:
        w()

    def low_sum(recv, sx, sy):
        parts = [jnp.where(exists(low, (sx, sy, sz)), recv[sz], zero) for sz in range(2)]
        return parts[0] + parts[1]

    low_x, low_y, low_xy = low_sum(tx_recv, 1, 0), low_sum(ty_recv, 0, 1), low_sum(txy_recv, 1, 1)
    zlow = jnp.where(has_low[2], z_recv[0, 0], zero)
    low_z = [zlow[:, 2 * tiles + n : 2 * tiles + n + 1] for n in range(block // 8)]
    own = spread_z + jnp.concatenate(low_z, axis=0) * take_first

    def spread_row(e, f):
        if e >= 0 and f >= 0:
            return own[e * ey + f : e * ey + f + 1]
        if f >= 0:
            return low_x[f : f + 1]
        return low_y[e : e + 1] if e >= 0 else low_xy

    columns = []
    for e in range(-1, ex):
        total = None
        for f in range(-1, ey):
            term = spread_row(e, f) * y_coef[f + 1]
            total = term if total is None else total + term
        columns.append(total)
    for i in range(nx):
        e, a = divmod(i, 4)
        if a == 0:
            mass = (columns[e + 1] + columns[e]) * jnp.float32(WN0)
        else:
            mass = columns[e + 1] * jnp.float32(WN[a])
        value = mass * first[0] + (end_yz + end_x) if i == 0 else mass + end_yz
        rows = slice(i * ny, (i + 1) * ny)
        diag[rows, :] = value
        scaled[rows, :] = work[rows, :] + value * adj[rows, :]

    ysums = element_lines([ys(adj, j) * ys(scaled, j) for j in range(ny)], ey)
    for f in range(8):
        lines[f * nx : (f + 1) * nx, :] = ysums[f] if f <= ey else jnp.zeros((nx, nz), jnp.float32)
    xsums = element_lines([lines[pl.ds(i, 8, stride=nx), :] for i in range(nx)], ex)
    packed = jnp.zeros((8, nz), jnp.float32)
    for e in range(ex + 1):
        packed = jnp.where(lane8 == e, xsums[e][:, 0:1] * jnp.float32(WEIGHTS[4]), packed)
    ez_send[...] = packed
    ezy_send[...] = packed[ey : ey + 1]
    e_got = []

    def send_sums(off, src, dst):
        e_got.append(message(src, dst, 19 + OFFSETS.index(off), off, -1))

    send_sums((1, 1, 1), ezy_send, ezy_recv.at[1])
    send_sums((0, 1, 1), ezy_send, ezy_recv.at[0])
    send_sums((1, 0, 1), ez_send, ez_recv.at[1])
    send_sums((0, 0, 1), ez_send, ez_recv.at[0])
    fill_faces(scaled, 1)
    got = send_faces(scaled, 1)

    loads[4].wait()
    zsums = dot(jnp.concatenate(xsums, axis=0), zred[...])
    e_own[...] = zsums
    for e in range(ex):
        ey_send[e : e + 1] = zsums[8 * e + ey : 8 * e + ey + 1]
    exy_send[...] = zsums[8 * ex + ey : 8 * ex + ey + 1]
    send_sums((1, 1, 0), exy_send, exy_recv)
    send_sums((0, 1, 0), ey_send, ey_recv)
    send_sums((1, 0, 0), e_own.at[8 * ex : 8 * ex + 8], ex_recv)

    own_terms(scaled)
    work[...] += diag[...] * scaled[...]
    for w in got:
        w()
    layer = halo_terms(1)
    for i in range(nx):
        rows = slice(i * ny, (i + 1) * ny)
        factor = mass_yz * jnp.float32(LUMPED[i % 4])
        if i == 0:
            factor = factor / first[0]
        prior[rows, :] = (work[rows, :] + layer(i)) * factor

    for copy, to, off in started:
        @pl.when(exists(to, off))
        def _():
            copy.wait_send()

    for w in e_got:
        w()
    row8 = lax.broadcasted_iota(jnp.int32, (8, ez), 0)
    at_end = lax.broadcasted_iota(jnp.int32, (1, ez), 1) == ez - 1

    def from_high(value, off):
        return jnp.where(exists(high, off), value, zero)

    for e in range(ex):
        total = e_own[8 * e : 8 * e + 8]
        side = from_high(ez_recv[0][:, e : e + 1], (0, 0, 1))
        corner = from_high(ezy_recv[0][:, e : e + 1], (0, 1, 1))
        above = from_high(ey_recv[e : e + 1], (0, 1, 0))
        if e == ex - 1:
            total = total + from_high(ex_recv[...], (1, 0, 0))
            side = side + from_high(ez_recv[1][:, ex : ex + 1], (1, 0, 1))
            corner = corner + from_high(ezy_recv[1][:, ex : ex + 1], (1, 1, 1))
            above = above + from_high(exy_recv[...], (1, 1, 0))
        above = above + jnp.where(at_end, corner, zero)
        total = total + jnp.where(at_end, side, zero) + jnp.where(row8 == ey - 1, above, zero)
        kgrad[e] = total[:ey] * (own_kappa[e] * jnp.float32(0.002))


def finish(prior, kgrad, prior_out, kgrad_out, sem):
    copies = [
        pltpu.make_async_copy(src, dst, sem.at[n])
        for n, (src, dst) in enumerate(((prior, prior_out), (kgrad, kgrad_out)))
    ]
    for copy in copies:
        copy.start()
    for copy in copies:
        copy.wait()


def on_device(sizes, adjoint, element_zone_index, kappa_table):
    nx, ny, nz = adjoint.shape
    elems = ex, ey, ez = element_zone_index.shape
    consts = [jnp.asarray(c) for c in constants(ez)]
    f32 = jnp.float32
    vmem = pl.BlockSpec(memory_space=pltpu.VMEM)
    hbm = pl.BlockSpec(memory_space=pltpu.HBM)
    prior, kgrad = pl.pallas_call(
        functools.partial(kernel, sizes, elems),
        out_shape=(pltpu.VMEM((nx * ny, nz), f32), pltpu.VMEM((ex, ey, ez), f32)),
        in_specs=[hbm] * (3 + len(consts)),
        out_specs=(vmem, vmem),
        scratch_shapes=[
            pltpu.VMEM((nx * ny, nz), f32),
            pltpu.VMEM((ex, ey, ez), jnp.int32),
            pltpu.SMEM(kappa_table.shape, f32),
            pltpu.VMEM(consts[0].shape, f32),
            pltpu.VMEM(consts[1].shape, f32),
            pltpu.VMEM(consts[2].shape, f32),
            pltpu.VMEM((nx * ny, nz), f32),
            pltpu.VMEM((nx * ny, nz), f32),
            pltpu.VMEM((nx * ny, nz), f32),
            pltpu.VMEM((8 * nx, nz), f32),
            pltpu.VMEM((2, 3, ny, nz), f32),
            pltpu.VMEM((2, 4, ny, nz), f32),
            pltpu.VMEM((2, 8, nz), f32),
            pltpu.VMEM((2, 2, 8, nz), f32),
            pltpu.VMEM((2, ey, nz), f32),
            pltpu.VMEM((2, ex, nz), f32),
            pltpu.VMEM((2, 1, nz), f32),
            pltpu.VMEM((2, ey, nz), f32),
            pltpu.VMEM((2, ex, nz), f32),
            pltpu.VMEM((2, 1, nz), f32),
            pltpu.VMEM((8 * ex + 8, ez), f32),
            pltpu.VMEM((ex, ez), f32),
            pltpu.VMEM((1, ez), f32),
            pltpu.VMEM((8, nz), f32),
            pltpu.VMEM((1, nz), f32),
            pltpu.VMEM((8, ez), f32),
            pltpu.VMEM((ex, ez), f32),
            pltpu.VMEM((1, ez), f32),
            pltpu.VMEM((2, 8, nz), f32),
            pltpu.VMEM((2, 1, nz), f32),
            pltpu.SemaphoreType.DMA((6,)),
            pltpu.SemaphoreType.DMA((26,)),
            pltpu.SemaphoreType.DMA((26,)),
        ],
        compiler_params=pltpu.CompilerParams(
            collective_id=0, has_side_effects=True
        ),
        name="bilaplacian",
    )(adjoint.reshape(nx * ny, nz), element_zone_index, kappa_table, *consts)
    prior, kgrad = pl.pallas_call(
        finish,
        out_shape=(
            jax.ShapeDtypeStruct((nx * ny, nz), f32),
            jax.ShapeDtypeStruct((ex, ey, ez), f32),
        ),
        in_specs=[vmem, vmem],
        out_specs=(hbm, hbm),
        scratch_shapes=[pltpu.SemaphoreType.DMA((2,))],
        name="finish",
    )(*(pltpu.with_memory_space_constraint(r, pltpu.VMEM) for r in (prior, kgrad)))
    return prior.reshape(nx, ny, nz), kgrad


def solution(mesh):
    sizes = tuple(mesh.shape[a] for a in AXES)
    return jax.shard_map(
        functools.partial(on_device, sizes), mesh=mesh,
        in_specs=(P("gx", "gy", "gz"), P("gx", "gy", "gz"), P()),
        out_specs=(P("gx", "gy", "gz"), P("gx", "gy", "gz")), check_vma=False,
    )
```
